32 devices in a mesh: dom: 16 (over z, x, core), rep: 2 (over y).
Axes of the slice: x: 2, y: 2, z: 4, core: 2. Of those that a mesh axis runs over, the one named last changes fastest.
Arguments:
- seed_feat: bfloat16 [1024, 512, 128], P('dom', 'rep'), may hold values from -6 to 6
- table: bfloat16 [8192, 512, 128], P('dom', 'rep'), may hold values from -6 to 6
- nbr_owner: int32 [1024, 8], P('dom'), may hold values from 0 to 15, all different within a row; in each aligned block of 64 rows (0 to 63, 64 to 127, ...) at most 48 rows name the same one
- nbr_local: int32 [1024, 8], P('dom'), may hold values from 0 to 511
- edge_words: int32 [1024, 8, 8, 128], P('dom'), may hold values from 0 to 65535
- weight: bfloat16 [512, 512], P('rep'), may hold values from -0.25 to 0.25
Outputs:
- output: bfloat16 [131072, 512], P(('dom', 'rep'))
The draws below stay inside these ranges and needn't reach their ends.
Inputs may be any that keep to these rules, and one draw needn't show every extreme that they name: `nbr_owner`: each row names 8 different partitions; among the rows of one index of dom no partition is named more than 48 times, a bound that some block reaches.
All inputs are finite; a program needn't handle non-finite values.
Results may differ from the reference program's by a relative error of at most 0.005.
Values may be sent and summed in bfloat16 or wider, within the bound.
No kernel may reach another device: no remote copies, remote signals or barrier semaphores. Data moves between devices by JAX's collectives and lax.ppermute only.
A program may use at most 320 MiB of HBM per device.

```python
import math
import jax
import jax.numpy as jnp
import numpy as np
from jax import lax

D = 512
NODE_BLK = 128
K = 8
SEED_DEV = 64
BLK_DEV = 512
CAP = 48
SEEDS = 1024
NBLK = 8192
N_DOM = 16


def place_ends(values, stream_key, low, top_value):
    dims = values.shape
    place = [jax.random.randint(jax.random.fold_in(stream_key, axis), (), 0, dims[axis]) for axis in range(len(dims))]
    values = values.at[tuple(place)].set(low)
    longest = dims.index(max(dims))
    place[longest] = (place[longest] + 1) % dims[longest]
    return values.at[tuple(place)].set(top_value)


def shard_levels(own_key, shape, cuts, low, top_value):
    def one(dim, parts):
        heights = jax.random.uniform(jax.random.fold_in(jax.random.fold_in(own_key, 6), dim), (parts,), jnp.float32, low / len(cuts), top_value / len(cuts))
        return jnp.repeat(jnp.exp(heights), shape[dim] // parts).reshape((-1,) + (1,) * (len(shape) - dim - 1))

    level = one(*cuts[0])
    for cut in cuts[1:]:
        level = level * one(*cut)
    return level


def shared_out(key, own, number, rows, count, top, most, slope):
    ranking = jax.random.permutation(key, count)
    crowded, common = load_shares(count, rows * top, most, slope, True), load_shares(count, rows * top, most, slope, False)
    places = jnp.arange(count)

    def named(sizes, rotation):
        used = int((sizes > 0).sum())
        fixed = max(1, used // 4)
        passed = fixed + (places - fixed + rotation * (used - fixed)) % max(1, count - fixed)
        return jnp.zeros((count,), jnp.int32).at[ranking[jnp.where(places < fixed, places, passed)]].set(jnp.asarray(sizes, jnp.int32))

    sizes = jnp.where(number % 4 == 0, named(crowded, number // 4), named(common, number - number // 4 - 1))
    mixed = jax.random.permutation(jax.random.fold_in(own, 3), count)
    giver, receiver = mixed[0:count // 2 * 2:2], mixed[1:count // 2 * 2:2]
    room = jnp.minimum(sizes[giver] - 1, most - sizes[receiver]) // 2
    room = jnp.where((giver == ranking[0]) | (receiver == ranking[0]) | (sizes[receiver] == 0), 0, jnp.maximum(room, 0))
    passed = jax.random.randint(jax.random.fold_in(own, 4), (count // 2,), 0, 1 << 20) % (room + 1)
    sizes = sizes.at[giver].add(-passed).at[receiver].add(passed)
    members = jnp.searchsorted(jnp.cumsum(sizes), jnp.arange(rows * top), side="right").astype(jnp.int32)
    grid = members.reshape(top, rows).T
    grid = grid[jax.random.permutation(jax.random.fold_in(own, 1), rows)]
    rotation = jax.random.randint(jax.random.fold_in(own, 2), (rows, 1), 0, top)
    return jnp.take_along_axis(grid, (jnp.arange(top)[None, :] + rotation) % top, axis=1)


def load_shares(count, total, most, lean, full):
    weights = [(1 << 20) // math.isqrt(standing ** lean) + 1 for standing in range(1, count + 1)]
    largest = most if full else min(most, max(-(-total // count), total * weights[0] // sum(weights)))
    least = 1 if total - largest >= count - 1 else 0
    holding, surplus = [largest] + [least] * (count - 1), total - largest - least * (count - 1)
    while surplus > 0:
        free = [i for i in range(1, count) if holding[i] < largest] or [i for i in range(1, count) if holding[i] < most]
        whole, left = sum([weights[i] for i in free]), surplus
        for i in free:
            addition = min(most - holding[i], max(1, left * weights[i] // whole), surplus)
            holding[i] = holding[i] + addition
            surplus = surplus - addition
    return np.array(holding)


def noise(stream_key, dims, scale, bound, cuts=(), kind=jnp.bfloat16):
    entries = jax.random.normal(stream_key, dims, jnp.float32) * scale
    if len(cuts) > 0:
        entries = shard_levels(stream_key, dims, cuts, -0.22, 0.18) * entries
    return jnp.clip(entries, min=-bound, max=bound).astype(kind)


def setup_inputs(seed: int = 0) -> dict:
    keys = jax.random.split(jax.random.key(seed), 7)
    seed_feat = noise(keys[0], (SEEDS, D, NODE_BLK), 1.0, 6.0, ((0, 16), (1, 2)))
    table = noise(keys[1], (NBLK, D, NODE_BLK), 1.0, 6.0, ((0, 16), (1, 2)))
    nbr_owner_keys = jax.random.split(jax.random.fold_in(keys[2], 1), SEEDS // SEED_DEV)
    nbr_owner_turns = jax.random.permutation(jax.random.fold_in(keys[2], 3), SEEDS // SEED_DEV)
    nbr_owner = jax.vmap(lambda own, number: shared_out(jax.random.fold_in(keys[2], 2), own, number, SEED_DEV, N_DOM, K, CAP, 2))(nbr_owner_keys, nbr_owner_turns).reshape((SEEDS, K))
    nbr_local = place_ends(jax.random.randint(keys[3], (SEEDS, K), 0, BLK_DEV), jax.random.fold_in(keys[3], 1), 0, BLK_DEV - 1).astype(jnp.int32)
    edge_words = place_ends(jax.random.randint(keys[4], (SEEDS, K, NODE_BLK // 16, NODE_BLK), 0, 65536), jax.random.fold_in(keys[4], 1), 0, 65535).astype(jnp.int32)
    weight = noise(keys[5], (D, D), D ** -0.5, 0.25, ((0, 2),))
    return {"seed_feat": seed_feat, "table": table, "nbr_owner": nbr_owner, "nbr_local": nbr_local, "edge_words": edge_words, "weight": weight}


def reference(seed_feat, table, nbr_owner, nbr_local, edge_words, weight):
    shifts = jnp.arange(16, dtype=jnp.int32)

    def per_seed(packed):
        self_rows, owners, local_ids, words_row = packed
        block_ids = (owners * BLK_DEV + local_ids).astype(jnp.int32)
        neighbours = table[block_ids].astype(jnp.float32)
        edge_bits = jnp.bitwise_and(jnp.right_shift(words_row[:, :, None, :], shifts[None, None, :, None]), 1)
        edge_bits = edge_bits.reshape(K, NODE_BLK, NODE_BLK)
        degree = lax.optimization_barrier(jnp.sum(edge_bits, axis=(0, 2))).astype(jnp.float32)
        summed = jnp.einsum('kcj,kij->ci', neighbours, edge_bits.astype(jnp.float32))
        combined = (self_rows.astype(jnp.float32) + summed / jnp.sqrt(1.0 + degree)[None, :]).astype(jnp.bfloat16)
        mixed = jnp.dot(combined.T, weight, preferred_element_type=jnp.float32)
        return jnp.maximum(mixed, 0.0).astype(jnp.bfloat16)
    result = lax.map(per_seed, (seed_feat, nbr_owner, nbr_local, edge_words))
    return result.reshape(SEEDS * NODE_BLK, D)
```

```python
import jax
import jax.numpy as jnp
from jax import lax
from jax.experimental import pallas as pl
from jax.experimental.pallas import tpu as pltpu
from jax.sharding import PartitionSpec as P


NX, NC = 2, 2
GROUP = 8


def spread_kernel(owner_ref, place_ref, words_ref, out_ref):
    z, x, rot = place_ref[0], place_ref[1], place_ref[2]
    seeds, fanout = owner_ref.shape
    half = out_ref.shape[3]
    out_ref[...] = jnp.zeros(out_ref.shape, out_ref.dtype)

    def body(s, carry):
        src = lax.rem(s + rot, seeds)
        h = s // half
        t = s - h * half
        for k in range(fanout):
            o = owner_ref[src, k]
            m = jnp.bitwise_xor(o // (NX * NC), z)
            n = jnp.bitwise_xor(lax.rem(o // NC, NX), x)
            out_ref[m, h, n, t, lax.rem(o, NC)] = words_ref[src, k].astype(out_ref.dtype)
        return carry

    lax.fori_loop(0, seeds, body, 0)


def spread(nbr_owner, place, edge_words, nz, halves):
    seeds, fanout, nw, nj = edge_words.shape
    shape = (nz, halves, NX, seeds // halves, NC, nw, nj)
    return pl.pallas_call(
        spread_kernel,
        out_shape=jax.ShapeDtypeStruct(shape, jnp.int16),
        grid_spec=pltpu.PrefetchScalarGridSpec(
            num_scalar_prefetch=2,
            grid=(1,),
            in_specs=[pl.BlockSpec(edge_words.shape, lambda i, *_: (0, 0, 0, 0))],
            out_specs=pl.BlockSpec(shape, lambda i, *_: (0,) * 7),
        ),
        name="spread",
    )(nbr_owner, place, edge_words)


def unpack(words):
    nw, nj = words.shape
    spread_words = jnp.broadcast_to(words.astype(jnp.int32)[:, None, :], (nw, 16, nj)).reshape(nw * 16, nj)
    bit = jnp.bitwise_and(lax.broadcasted_iota(jnp.int32, (nw * 16, nj), 0), 15)
    return jnp.bitwise_and(jnp.right_shift(spread_words, bit), 1).astype(jnp.float32).astype(jnp.bfloat16)


def partial_kernel(ids_ref, core_ref, *refs):
    tables, (fetched_ref, mask_ref, out_ref) = refs[:GROUP], refs[GROUP:]
    core = core_ref[0]
    for g in range(GROUP):
        bits = jnp.concatenate([unpack(mask_ref[g, core]), unpack(mask_ref[g, 1 - core])], axis=1)
        rows = jnp.concatenate([tables[g][0], fetched_ref[0, g]], axis=1)
        acc = lax.dot_general(rows, bits, (((1,), (1,)), ((), ())), preferred_element_type=jnp.float32)
        out_ref[g] = acc.astype(out_ref.dtype)


def partial_sum(ids, core, table, fetched, masks, n, dtype):
    count = ids.shape[0]
    _, channels, nj = table.shape
    nw = masks.shape[2]

    def table_spec(g):
        return pl.BlockSpec((1, channels, nj), lambda i, ids_ref, core_ref, g=g: (ids_ref[i * GROUP + g], 0, 0))

    return pl.pallas_call(
        partial_kernel,
        out_shape=jax.ShapeDtypeStruct((count, channels, nw * 16), dtype),
        grid_spec=pltpu.PrefetchScalarGridSpec(
            num_scalar_prefetch=2,
            grid=(count // GROUP,),
            in_specs=[table_spec(g) for g in range(GROUP)]
            + [
                pl.BlockSpec((1, GROUP, channels, nj), lambda i, *_: (n, i, 0, 0)),
                pl.BlockSpec((GROUP, NC, nw, nj), lambda i, *_: (i, 0, 0, 0)),
            ],
            out_specs=pl.BlockSpec((GROUP, channels, nw * 16), lambda i, *_: (i, 0, 0)),
        ),
        name="partial_sum",
    )(ids, core, *([table] * GROUP), fetched, masks)


def local(seed_feat, table, nbr_owner, nbr_local, edge_words, weight):
    seeds, fanout = nbr_owner.shape
    channels, node_count = seed_feat.shape[1:]
    dom = lax.axis_size("dom")
    reps = lax.axis_size("rep")
    nz = dom // (NX * NC)
    halves = 2
    half = seeds // halves
    part = seeds // reps
    p = lax.axis_index("dom")
    r = lax.axis_index("rep")
    z, x, c = p // (NX * NC), (p // NC) % NX, p % NC
    rot = ((r + 1) % reps) * part

    def pairs(move):
        out = []
        for q in range(dom):
            to = move(q // (NX * NC), (q // NC) % NX, q % NC)
            if to is not None:
                out.append((q, (to[0] * NX + to[1]) * NC + to[2]))
        return out

    def xor_move(m, n, e):
        return pairs(lambda a, b, d: (a ^ m, b ^ n, d ^ e))

    def line(step, sign):
        return pairs(lambda a, b, d: (a + sign, b, d) if 0 <= a + sign * step < nz else None)

    place = jnp.stack([z, x, rot]).astype(jnp.int32)
    sent_masks = spread(nbr_owner, place, edge_words, nz, halves)
    masks = {}
    order = [(m, h) for m in range(nz - 1, -1, -1) for h in range(halves)]
    for m, h in order:
        for n in (1, 0):
            own = sent_masks[m, h, n]
            masks[m, h, n] = own if m == 0 and n == 0 else lax.ppermute(own, "dom", xor_move(m, n, 0))

    hit = nbr_owner[:, :, None] == jnp.arange(dom, dtype=jnp.int32)[None, None, :]
    ids = jnp.sum(jnp.where(hit, nbr_local[:, :, None], 0), axis=1)
    ids = jnp.concatenate([ids, ids], axis=0)
    ids = lax.dynamic_slice(ids, (rot, 0), (seeds, dom)).T
    asked = lax.all_to_all(ids, "dom", split_axis=0, concat_axis=0, tiled=True)
    q = jnp.arange(dom, dtype=jnp.int32)
    asked = jnp.take(asked, jnp.bitwise_xor(q, p), axis=0, mode="clip").reshape(nz, NX, NC, halves, half)

    core = c.reshape(1).astype(jnp.int32)
    swap = xor_move(0, 0, 1)
    cross = xor_move(0, 1, 0)
    sums, crossed = {}, {}
    for m, h in order:
        rows = jnp.take(table, asked[m, :, 1, h].reshape(NX * half), axis=0, mode="clip")
        fetched = lax.ppermute(rows.reshape(NX, half, channels, node_count), "dom", swap)
        away = partial_sum(asked[m, 1, 0, h], core, table, fetched, masks[m, h, 1], 1, jnp.bfloat16)
        crossed[m, h] = lax.ppermute(away, "dom", cross)
        sums[m, h] = partial_sum(asked[m, 0, 0, h], core, table, fetched, masks[m, h, 0], 0, jnp.float32)

    degree_bits = jnp.bitwise_and(
        jnp.right_shift(edge_words[:, :, :, None, :], jnp.arange(16, dtype=jnp.int32)[None, None, None, :, None]), 1
    )
    degree = jnp.sum(degree_bits, axis=(1, 4)).reshape(seeds, node_count).astype(jnp.float32)
    root = jnp.sqrt(1.0 + degree)

    def both(m, h):
        return sums[m, h] + crossed[m, h].astype(jnp.float32)

    def at_distance(step, sign, h):
        target = z + sign * step
        m = jnp.bitwise_xor(target, z)
        kinds = sorted({(a ^ (a + sign * step)) for a in range(nz) if 0 <= a + sign * step < nz})
        value = both(kinds[0], h)
        for k in kinds[1:]:
            value = jnp.where(m == k, both(k, h), value)
        return value

    arrived = {}
    for step in range(nz - 1, 0, -1):
        for h in range(halves):
            for sign in (1, -1):
                value = at_distance(step, sign, h)
                if step < nz - 1:
                    value = value + arrived[sign, h].astype(jnp.float32)
                arrived[sign, h] = lax.ppermute(value.astype(jnp.bfloat16), "dom", line(step, sign))

    weights = {0: weight}
    for j in range(1, reps):
        weights[j] = lax.ppermute(weight, "rep", [(a, (a - j) % reps) for a in range(reps)])

    mixed = []
    for h in range(halves):
        summed = both(0, h) + arrived[1, h].astype(jnp.float32) + arrived[-1, h].astype(jnp.float32)
        start = (rot + h * half) % seeds
        own = lax.dynamic_slice(seed_feat, (start, 0, 0), (half, channels, node_count)).astype(jnp.float32)
        scale = lax.dynamic_slice(root, (start, 0), (half, node_count))
        mixed.append((own + summed / scale[:, None, :]).astype(jnp.bfloat16))

    def group(j):
        return mixed[j * part // half] if part == half else jnp.concatenate(mixed, axis=0)[j * part : (j + 1) * part]

    total = None
    pieces = [(0, group(reps - 1))]
    for j in range(reps - 1):
        pieces.append(((reps - 1 - j) % reps, lax.ppermute(group(j), "rep", [(a, (a + 1 + j) % reps) for a in range(reps)])))
    for j, piece in pieces:
        product = jnp.einsum("sci,co->sio", piece, weights[j], preferred_element_type=jnp.float32)
        total = product if total is None else total + product
    return jnp.maximum(total, 0.0).astype(jnp.bfloat16).reshape(part * node_count, weight.shape[1])


def solution(mesh):
    placed = (
        P("dom", "rep", None),
        P("dom", "rep", None),
        P("dom", None),
        P("dom", None),
        P("dom", None, None, None),
        P("rep", None),
    )
    return jax.shard_map(
        local, mesh=mesh, in_specs=placed, out_specs=P(("dom", "rep"), None), check_vma=False
    )
```
